32 devices in a mesh: tm: 32 (over z, y, x, core).
Axes of the slice: x: 2, y: 2, z: 4, core: 2. Of those that a mesh axis runs over, the one named last changes fastest.
Arguments:
- wrapped: float32 [4096, 3, 512], P('tm'), may hold values from 0 to 1, as said below
- crossings: int32 [4096, 3, 512], P('tm'), may hold values from -1 to 1, as said below
- box_size: float32 [3], replicated, may hold values from 4 to 12
Outputs:
- msd: float32 [512, 128], P('tm')
The draws below stay inside these ranges and needn't reach their ends.
Inputs may be any that keep to these rules, and one draw needn't show every extreme that they name: `wrapped`: scaled coordinates within the unit cell. per-frame crossings, one of -1, 0, 1; most entries are 0.
All inputs are finite; a program needn't handle non-finite values.
Results may differ from the reference program's by a relative error of at most 0.0003.
Values sent between devices are 32-bit elements; how exact they have to be, the bound alone decides.
A program may use at most 64 MiB of HBM per device.

```python
import math
import jax
import jax.numpy as jnp
from jax import lax

ATOMS = 512
LAGS = 128
NT = 4096


def draw_wrapped(key, part):
    base_key, jitter_key = jax.random.split(jax.random.fold_in(key, 11))
    base = jax.random.uniform(base_key, (1, 3, ATOMS), jnp.float32)
    jitter = 0.08 * jax.random.normal(jitter_key, (NT, 3, ATOMS), jnp.float32)
    return jnp.mod(base + jitter, 1.0)


def draw_crossings(key, part):
    rolls = jax.random.randint(jax.random.fold_in(key, 23), (NT, 3, ATOMS), 0, 256, dtype=jnp.int32)
    upward = jnp.where(rolls == 0, 1, 0).astype(jnp.int32)
    downward = jnp.where(rolls == 255, 1, 0).astype(jnp.int32)
    return upward - downward


def setup_inputs(seed: int = 0) -> dict:
    key_list = jax.random.split(jax.random.key(seed), 4)
    wrapped = draw_wrapped(jax.random.fold_in(key_list[3], 71), 0)
    crossings = draw_crossings(jax.random.fold_in(key_list[3], 71), 0)
    box_size = jnp.clip(jnp.exp(jax.random.uniform(key_list[2], (3,), jnp.float32, math.log(4.0), math.log(12.0))), 4.0, 12.0)
    return {"wrapped": wrapped, "crossings": crossings, "box_size": box_size}


def reference(wrapped, crossings, box_size):
    image = jnp.cumsum(crossings, axis=0)
    unwrapped = (wrapped + image.astype(jnp.float32)) * box_size[None, :, None]
    total_frames = unwrapped.shape[0]
    atom_count = unwrapped.shape[2]
    frame_ids = jnp.arange(total_frames, dtype=jnp.int32)

    def per_block(first_atom):
        block = lax.dynamic_slice_in_dim(unwrapped, first_atom, 128, 2)
        extended = jnp.concatenate([block, jnp.zeros((LAGS, 3, 128), jnp.float32)], axis=0)

        def per_lag(lag_step):
            window = lax.dynamic_slice_in_dim(extended, lag_step, total_frames, 0)
            moved = window - block
            squares = jnp.sum(moved * moved, axis=1)
            in_range = (frame_ids + lag_step) < total_frames
            return jnp.sum(jnp.where(in_range[:, None], squares, jnp.float32(0.0)), axis=0)

        return lax.map(per_lag, jnp.arange(LAGS, dtype=jnp.int32))

    parts = lax.map(per_block, jnp.arange(atom_count // 128, dtype=jnp.int32) * 128)
    lag_sum = jnp.transpose(parts, (1, 0, 2)).reshape(LAGS, atom_count)
    divisor = (total_frames - jnp.arange(LAGS, dtype=jnp.int32)).astype(jnp.float32)
    return (lag_sum / divisor[:, None]).T
```

```python
import functools

import jax
import jax.numpy as jnp
import numpy as np
from jax import lax
from jax.experimental import pallas as pl
from jax.experimental.pallas import tpu as pltpu
from jax.sharding import PartitionSpec as P

LAGS = 128
LANES = 128
SUB = 8
SLOTS = 4
GROUP = 2 * SLOTS
MESH = pl.DeviceIdType.MESH
F32 = jnp.float32
BF16 = jnp.bfloat16


def split(x):
    hi = x.astype(BF16)
    return hi, (x - hi.astype(F32)).astype(BF16)


def kernel(n, wrapped, crossings, box, fwd_hbm, inv_hbm, out, wbuf, xbuf, sbuf, rbuf, fwd, inv, spec, zbuf,
           first_sq, last_sq, halo_sq, sum_sq, tbuf, part, load_sem, const_sem, send_sem, recv_sem, pass_sem,
           part_send, part_recv):
    dims, frames = wbuf.shape[:2]
    per_owner = out.shape[0]
    planes = n // GROUP
    quads = n // SLOTS
    width = 2 * per_owner
    sub_planes = LANES // (SLOTS * width)
    me = lax.axis_index("tm")
    plane = me // GROUP
    j = me % GROUP
    chip, core = j // 2, j % 2
    quad = 2 * plane + core
    slot = j % SLOTS
    is_last = quad == quads - 1

    def device(q, i):
        return GROUP * (q // 2) + 2 * i + q % 2

    barrier = pltpu.get_barrier_semaphore()

    @pl.loop(1, GROUP)
    def _(o):
        pl.semaphore_signal(barrier, inc=1, device_id=(GROUP * plane + (j + o) % GROUP,), device_id_type=MESH)

    @pl.loop(1, planes)
    def _(o):
        far = GROUP * ((plane + o) % planes) + 2 * chip
        pl.semaphore_signal(barrier, inc=1, device_id=(far,), device_id_type=MESH)
        pl.semaphore_signal(barrier, inc=1, device_id=(far + 1,), device_id_type=MESH)

    def load(c, which):
        src, dst = ((wrapped, wbuf), (crossings, xbuf))[which]
        return pltpu.make_async_copy(src.at[c], dst.at[c], load_sem.at[c, which])

    for c in range(dims):
        load(c, 1).start()
    for c in range(dims):
        load(c, 0).start()
    const_copies = [pltpu.make_async_copy(fwd_hbm, fwd, const_sem.at[0]),
                    pltpu.make_async_copy(inv_hbm, inv, const_sem.at[1])]
    for copy in const_copies:
        copy.start()

    lane = lax.broadcasted_iota(jnp.int32, (SUB, LANES), 1)
    sub = lax.broadcasted_iota(jnp.int32, (SUB, LANES), 0)

    def swap(a, b, dist):
        low = (lane[0:1] & dist) == 0
        return (jnp.where(low, a, pltpu.roll(b, dist, 1)), jnp.where(low, pltpu.roll(a, LANES - dist, 1), b))

    def pack(groups):
        a = list(groups)
        for k in (0, 1):
            a[k], a[k + 2] = swap(a[k], a[k + 2], 2 * width)
        for k in (0, 2):
            a[k], a[k + 1] = swap(a[k], a[k + 1], width)
        return a

    ones = jnp.ones((SUB, frames), BF16)
    tri = (lax.broadcasted_iota(jnp.int32, (frames, frames), 1)
           <= lax.broadcasted_iota(jnp.int32, (frames, frames), 0)).astype(F32).astype(BF16)

    def rows(c):
        start = 0 if c == 0 else SUB + c * frames
        return pl.ds(start, SUB + (c + 1) * frames - start)

    def lanes(g):
        return pl.ds(g * LANES, LANES)

    for c in range(dims):
        load(c, 1).wait()
    totals = [jnp.dot(ones, xbuf[c].astype(F32).astype(BF16), preferred_element_type=F32) for c in range(dims)]
    groups = []
    for g in range(SLOTS):
        t = [v[:, g * LANES:(g + 1) * LANES] for v in totals]
        groups.append(jnp.where(sub == 0, t[0], jnp.where(sub == 1, t[1], t[2])))
    for i, v in enumerate(pack(groups)):
        sbuf[i, 0:SUB, :] = v

    own_quad = 2 * plane + j // SLOTS

    def exchange(c, o):
        i = 2 * ((chip // 2 + o // 2) % 2) + (chip + o) % 2
        dst = device(own_quad, i)
        src, to = sbuf.at[i, rows(c), :], rbuf.at[slot, rows(c), :]
        remote = pltpu.make_async_remote_copy(
            src_ref=src, dst_ref=to, send_sem=send_sem.at[o, c], recv_sem=recv_sem.at[slot, c],
            device_id=(dst,), device_id_type=MESH)
        return dst == me, remote, pltpu.make_async_copy(src, to, recv_sem.at[slot, c])

    for c in range(dims):
        load(c, 0).wait()
        counts = jnp.dot(tri, xbuf[c].astype(F32).astype(BF16), preferred_element_type=F32)
        wbuf[c] = wbuf[c] + counts
        for r in range(0, frames, SUB):
            for i, v in enumerate(pack([wbuf[c, r:r + SUB, lanes(g)] for g in range(SLOTS)])):
                sbuf[i, SUB + c * frames + r:SUB + c * frames + r + SUB, :] = v
        if c == 0:
            pl.semaphore_wait(barrier, GROUP - 1 + 2 * (planes - 1))
        for o in (3, 1, 2):
            exchange(c, o)[1].start()
        mine, remote, local = exchange(c, 0)

        @pl.when(mine)
        def _():
            local.start()

        @pl.when(jnp.logical_not(mine))
        def _():
            remote.start()

    for copy in const_copies:
        copy.wait()

    def arrived(s, c):
        return pltpu.make_async_remote_copy(
            src_ref=sbuf.at[0, rows(c), :], dst_ref=rbuf.at[s, rows(c), :], send_sem=send_sem.at[0, c],
            recv_sem=recv_sem.at[s, c], device_id=(me,), device_id_type=MESH)

    def landed(s, c):
        pltpu.make_async_copy(sbuf.at[0, rows(c), :], rbuf.at[s, rows(c), :], recv_sem.at[s, c]).wait()

    def hand_on(c):
        return pltpu.make_async_remote_copy(
            src_ref=rbuf.at[0, rows(c), :], dst_ref=rbuf.at[SLOTS, rows(c), :], send_sem=pass_sem.at[c],
            recv_sem=recv_sem.at[SLOTS, c], device_id=(device(quad - 1, chip),), device_id_type=MESH)

    bins = LAGS
    half = bins // 2

    def position(s, c, off):
        u = rbuf[s, SUB + c * frames:SUB + (c + 1) * frames, :]
        return u * box[c] + off

    def total(s, c):
        return rbuf[s, c:c + 1, :]

    def transform(x):
        hi, lo = split(x)
        return jnp.dot(fwd[...], jnp.concatenate([hi, lo, hi], axis=0), preferred_element_type=F32)

    offs = {}

    def main(c):
        landed(0, c)

        @pl.when(quad > 0)
        def _():
            hand_on(c).start()

        for s in range(1, SLOTS):
            landed(s, c)
        mid = rbuf[2, SUB + c * frames:SUB + (c + 1) * frames, :]
        ref = jnp.sum(mid, axis=0, keepdims=True) * (-1.0 / frames)
        shift = [ref - total(1, c) - total(0, c), ref - total(1, c), ref, ref + total(2, c)]
        offs[c] = (ref + total(2, c) + total(3, c)) * box[c]
        xs = [position(s, c, shift[s] * box[c]) for s in range(SLOTS)]
        squares = [x * x for x in xs]
        all_sq = (squares[0] + squares[1]) + (squares[2] + squares[3])
        if c == 0:
            first_sq[...] = squares[0]
            last_sq[...] = squares[3]
            sum_sq[...] = all_sq
        else:
            first_sq[...] = first_sq[...] + squares[0]
            last_sq[...] = last_sq[...] + squares[3]
            sum_sq[...] = sum_sq[...] + all_sq
        for s in range(SLOTS):
            spec[c, s] = transform(xs[s])
        for sign, base in ((1, 0), (-1, half)):
            @pl.loop(0, half // SUB)
            def _(r):
                re_rows = pl.ds(pl.multiple_of(base + r * SUB, SUB), SUB)
                im_rows = pl.ds(pl.multiple_of(bins + base + r * SUB, SUB), SUB)
                res = [spec[c, s, re_rows, :] for s in range(SLOTS)]
                ims = [spec[c, s, im_rows, :] for s in range(SLOTS)]
                z_re = z_im = None
                for s in range(SLOTS):
                    if s < SLOTS - 1:
                        y_re = res[s] + ims[s + 1] if sign > 0 else res[s] - ims[s + 1]
                        y_im = ims[s] - res[s + 1] if sign > 0 else ims[s] + res[s + 1]
                        p_re = res[s] * y_re + ims[s] * y_im
                        p_im = res[s] * y_im - ims[s] * y_re
                        z_im = p_im if z_im is None else z_im + p_im
                    else:
                        p_re = res[s] * res[s] + ims[s] * ims[s]
                    z_re = p_re if z_re is None else z_re + p_re
                if c == 0:
                    zbuf[re_rows, :] = z_re
                    zbuf[im_rows, :] = z_im
                else:
                    zbuf[re_rows, :] = zbuf[re_rows, :] + z_re
                    zbuf[im_rows, :] = zbuf[im_rows, :] + z_im

    def halo(c):
        off = offs[c]

        @pl.when(jnp.logical_not(is_last))
        def _():
            landed(SLOTS, c)
            x = position(SLOTS, c, off)
            if c == 0:
                halo_sq[...] = x * x
            else:
                halo_sq[...] = halo_sq[...] + x * x
            spec[c, 0] = transform(x)
            for sign, base in ((1, 0), (-1, half)):
                @pl.loop(0, half // SUB)
                def _(r):
                    re_rows = pl.ds(pl.multiple_of(base + r * SUB, SUB), SUB)
                    im_rows = pl.ds(pl.multiple_of(bins + base + r * SUB, SUB), SUB)
                    x_re, x_im = spec[c, SLOTS - 1, re_rows, :], spec[c, SLOTS - 1, im_rows, :]
                    y_re, y_im = spec[c, 0, im_rows, :], spec[c, 0, re_rows, :]
                    if sign > 0:
                        zbuf[re_rows, :] = zbuf[re_rows, :] + (x_re * y_re - x_im * y_im)
                        zbuf[im_rows, :] = zbuf[im_rows, :] - (x_re * y_im + x_im * y_re)
                    else:
                        zbuf[re_rows, :] = zbuf[re_rows, :] - (x_re * y_re - x_im * y_im)
                        zbuf[im_rows, :] = zbuf[im_rows, :] + (x_re * y_im + x_im * y_re)

    @pl.when(is_last)
    def _():
        halo_sq[...] = jnp.zeros_like(halo_sq)

    main(0)
    main(1)
    halo(0)
    main(2)
    halo(1)
    halo(2)

    z_hi, z_lo = split(zbuf[...])
    w_hi, w_lo = split(halo_sq[...] - first_sq[...])
    v_hi, v_lo = split(jnp.where(is_last, -last_sq[...], 0.0))
    lag_sum = jnp.dot(inv[...], jnp.concatenate([z_hi, z_lo, z_hi, w_hi, w_lo, v_hi, v_lo], axis=0),
                      preferred_element_type=F32)
    lag_sum = lag_sum + 2.0 * jnp.sum(sum_sq[...], axis=0, keepdims=True)
    by_atom = lag_sum.T
    for g in range(SLOTS):
        for p in range(sub_planes):
            for k in range(2):
                first = p * SLOTS * width + g * width + k * per_owner
                tbuf[2 * (g * sub_planes + p) + k] = by_atom[first:first + per_owner, :]

    @pl.loop(0, quads)
    def _(q):
        @pl.when(q != quad)
        def _():
            pltpu.make_async_remote_copy(
                src_ref=tbuf.at[q], dst_ref=part.at[quad], send_sem=part_send, recv_sem=part_recv,
                device_id=(device(q, chip),), device_id_type=MESH).start()

    part[quad] = tbuf[quad]
    others = pl.ds(0, quads - 1)
    pltpu.make_async_remote_copy(
        src_ref=tbuf.at[others], dst_ref=part.at[others], send_sem=part_send, recv_sem=part_recv,
        device_id=((me + 1) % n,), device_id_type=MESH).wait()
    out[...] = jnp.sum(part[...], axis=0)

    for c in range(dims):
        for o in (3, 1, 2):
            exchange(c, o)[1].wait_send()
        mine, remote, local = exchange(c, 0)

        @pl.when(jnp.logical_not(mine))
        def _():
            remote.wait_send()

        @pl.when(quad > 0)
        def _():
            hand_on(c).wait_send()


def tables(frames):
    f = np.concatenate([np.arange(0, LAGS, 2), np.arange(1, LAGS, 2)]) + 0.5
    t = np.arange(frames)
    angle = 2.0 * np.pi * f[:, None] * t[None, :] / (2 * LAGS)
    fwd = np.concatenate([np.cos(angle), -np.sin(angle)], axis=0).astype(np.float32)
    back = (2.0 * np.pi * f[None, :] * np.arange(LAGS)[:, None]) / (2 * LAGS)
    inv = np.concatenate([np.cos(back), -np.sin(back)], axis=1) * (-2.0 / LAGS)
    inv = inv.astype(np.float32)

    def halves(x):
        hi = x.astype(jnp.bfloat16)
        return hi, (x - hi.astype(np.float32)).astype(jnp.bfloat16)

    k = np.arange(LAGS)[:, None]
    low = (t[None, :] < k).astype(jnp.bfloat16)
    high = (t[None, :] >= frames - k).astype(jnp.bfloat16)
    f_hi, f_lo = halves(fwd)
    i_hi, i_lo = halves(inv)
    return (np.concatenate([f_hi, f_hi, f_lo], axis=1),
            np.concatenate([i_hi, i_hi, i_lo, low, low, high, high], axis=1))


def on_device(n, wrapped, crossings, box_size):
    frames, dims, atoms = wrapped.shape
    per_owner = atoms // n
    quads = n // SLOTS
    assert frames == LAGS and atoms == SLOTS * LANES and n % GROUP == 0 and LANES % (GROUP * per_owner) == 0
    fwd, inv = tables(frames)
    any_spec = pl.BlockSpec(memory_space=pl.ANY)
    piece = SUB + dims * frames
    lag_sum = pl.pallas_call(
        functools.partial(kernel, n),
        out_shape=jax.ShapeDtypeStruct((per_owner, LAGS), F32),
        in_specs=[any_spec, any_spec, pl.BlockSpec(memory_space=pltpu.SMEM), any_spec, any_spec],
        out_specs=pl.BlockSpec(memory_space=pltpu.VMEM),
        scratch_shapes=[
            pltpu.VMEM((dims, frames, atoms), F32),
            pltpu.VMEM((dims, frames, atoms), jnp.int32),
            pltpu.VMEM((SLOTS, piece, LANES), F32),
            pltpu.VMEM((SLOTS + 1, piece, LANES), F32),
            pltpu.VMEM(fwd.shape, BF16),
            pltpu.VMEM(inv.shape, BF16),
            pltpu.VMEM((dims, SLOTS, 2 * LAGS, LANES), F32),
            pltpu.VMEM((2 * LAGS, LANES), F32),
            pltpu.VMEM((frames, LANES), F32),
            pltpu.VMEM((frames, LANES), F32),
            pltpu.VMEM((frames, LANES), F32),
            pltpu.VMEM((frames, LANES), F32),
            pltpu.VMEM((quads, per_owner, LAGS), F32),
            pltpu.VMEM((quads, per_owner, LAGS), F32),
            pltpu.SemaphoreType.DMA((dims, 2)),
            pltpu.SemaphoreType.DMA((2,)),
            pltpu.SemaphoreType.DMA((SLOTS, dims)),
            pltpu.SemaphoreType.DMA((SLOTS + 1, dims)),
            pltpu.SemaphoreType.DMA((dims,)),
            pltpu.SemaphoreType.DMA,
            pltpu.SemaphoreType.DMA,
        ],
        compiler_params=pltpu.CompilerParams(collective_id=0, has_side_effects=True),
    )(jnp.transpose(wrapped, (1, 0, 2)), jnp.transpose(crossings, (1, 0, 2)), box_size,
      jnp.asarray(fwd), jnp.asarray(inv))
    divisor = (n * frames - jnp.arange(LAGS, dtype=jnp.int32)).astype(F32)
    return lag_sum / divisor[None, :]


def solution(mesh):
    in_specs = (P("tm", None, None), P("tm", None, None), P())
    out_specs = P("tm", None)
    return jax.shard_map(
        functools.partial(on_device, mesh.shape["tm"]), mesh=mesh,
        in_specs=in_specs, out_specs=out_specs, check_vma=False)
```

```python
import functools

import jax
import jax.numpy as jnp
import numpy as np
from jax import lax
from jax.experimental import pallas as pl
from jax.experimental.pallas import tpu as pltpu
from jax.sharding import PartitionSpec as P

LAGS = 128
LANES = 128
SUB = 8
SLOTS = 4
GROUP = 2 * SLOTS
MESH = pl.DeviceIdType.MESH
F32 = jnp.float32
BF16 = jnp.bfloat16


def split(x):
    hi = x.astype(BF16)
    return hi, (x - hi.astype(F32)).astype(BF16)


def kernel(n, wrapped, crossings, box_hbm, fwd_hbm, inv_hbm, out, wbuf, xbuf, sbuf, rbuf, fwd, inv, spec, zbuf,
           first_sq, last_sq, halo_sq, sum_sq, tbuf, part, load_sem, const_sem, box, send_sem, recv_sem, pass_sem,
           part_send, part_recv, diag_sem, up_sem, down_sem):
    dims, frames = wbuf.shape[:2]
    per_owner = out.shape[0]
    planes = n // GROUP
    quads = n // SLOTS
    width = 2 * per_owner
    sub_planes = LANES // (SLOTS * width)
    me = lax.axis_index("tm")
    plane = me // GROUP
    j = me % GROUP
    chip, core = j // 2, j % 2
    quad = 2 * plane + core
    slot = j % SLOTS
    is_last = quad == quads - 1

    def device(q, i):
        return GROUP * (q // 2) + 2 * i + q % 2

    x, y = chip % 2, chip // 2
    partner = me + 1 - 2 * core

    def nearby(o, k):
        return GROUP * plane + 2 * (2 * ((y + o // 2) % 2) + (x + o) % 2) + k

    def signal(sem, dst):
        pl.semaphore_signal(sem, inc=1, device_id=(dst,), device_id_type=MESH)

    barrier = pltpu.get_barrier_semaphore()
    below, above = plane > 0, plane < planes - 1
    signal(barrier, partner)
    for k in range(2):
        signal(barrier, nearby(1, k))
        signal(barrier, nearby(2, k))

    @pl.when(below)
    def _():
        for k in range(2):
            signal(barrier, GROUP * (plane - 1) + 2 * chip + k)

    @pl.when(above)
    def _():
        for k in range(2):
            signal(barrier, GROUP * (plane + 1) + 2 * chip + k)

    greeted = 5 + 2 * jnp.where(below, 1, 0) + 2 * jnp.where(above, 1, 0)

    def spread(first, last):
        @pl.loop(first, last)
        def _(r):
            @pl.when(below)
            def _():
                signal(up_sem, me - GROUP)

            @pl.when(above)
            def _():
                signal(down_sem, me + GROUP)

            @pl.when(above)
            def _():
                pl.semaphore_wait(up_sem, 1)

            @pl.when(below)
            def _():
                pl.semaphore_wait(down_sem, 1)

    rounds = max(planes - 2, 0)

    def load(c, which):
        src, dst = ((wrapped, wbuf), (crossings, xbuf))[which]
        return pltpu.make_async_copy(src.at[c], dst.at[c], load_sem.at[c, which])

    load(0, 1).start()
    load(0, 0).start()
    for c in range(1, dims):
        load(c, 1).start()
    for c in range(1, dims):
        load(c, 0).start()
    const_copies = [pltpu.make_async_copy(fwd_hbm, fwd, const_sem.at[0]),
                    pltpu.make_async_copy(inv_hbm, inv, const_sem.at[1]),
                    pltpu.make_async_copy(box_hbm, box, const_sem.at[2])]
    for copy in const_copies:
        copy.start()

    lane = lax.broadcasted_iota(jnp.int32, (SUB, LANES), 1)
    sub = lax.broadcasted_iota(jnp.int32, (SUB, LANES), 0)

    def swap(a, b, dist):
        low = (lane[0:1] & dist) == 0
        return (jnp.where(low, a, pltpu.roll(b, dist, 1)), jnp.where(low, pltpu.roll(a, LANES - dist, 1), b))

    def pack(groups):
        a = list(groups)
        for k in (0, 1):
            a[k], a[k + 2] = swap(a[k], a[k + 2], 2 * width)
        for k in (0, 2):
            a[k], a[k + 1] = swap(a[k], a[k + 1], width)
        return a

    ones = jnp.ones((SUB, frames), BF16)
    tri = (lax.broadcasted_iota(jnp.int32, (frames, frames), 1)
           <= lax.broadcasted_iota(jnp.int32, (frames, frames), 0)).astype(F32).astype(BF16)

    def rows(c):
        return (pl.ds(0, frames), pl.ds(frames, SUB + frames), pl.ds(SUB + 2 * frames, frames))[c]

    def row0(c):
        return c * frames + (SUB if c > 0 else 0)

    def lanes(g):
        return pl.ds(g * LANES, LANES)

    own_quad = 2 * plane + j // SLOTS

    def exchange(c, o):
        i = 2 * ((chip // 2 + o // 2) % 2) + (chip + o) % 2
        dst = device(own_quad, i)
        src, to = sbuf.at[i, rows(c), :], rbuf.at[slot, rows(c), :]
        remote = pltpu.make_async_remote_copy(
            src_ref=src, dst_ref=to, send_sem=send_sem.at[o, c], recv_sem=recv_sem.at[slot, c],
            device_id=(dst,), device_id_type=MESH)
        return dst == me, remote, pltpu.make_async_copy(src, to, recv_sem.at[slot, c])

    for c in range(dims):
        if c == 1:
            for k in range(1, dims):
                load(k, 1).wait()
            totals = [jnp.dot(ones, xbuf[c].astype(F32).astype(BF16), preferred_element_type=F32) for c in range(dims)]
            groups = []
            for g in range(SLOTS):
                t = [v[:, g * LANES:(g + 1) * LANES] for v in totals]
                groups.append(jnp.where(sub == 0, t[0], jnp.where(sub == 1, t[1], t[2])))
            for i, v in enumerate(pack(groups)):
                sbuf[i, frames:frames + SUB, :] = v
        if c == 0:
            load(c, 1).wait()
        load(c, 0).wait()
        counts = jnp.dot(tri, xbuf[c].astype(F32).astype(BF16), preferred_element_type=F32)
        wbuf[c] = wbuf[c] + counts
        for r in range(0, frames, SUB):
            for i, v in enumerate(pack([wbuf[c, r:r + SUB, lanes(g)] for g in range(SLOTS)])):
                sbuf[i, row0(c) + r:row0(c) + r + SUB, :] = v
        if c == 0:
            pl.semaphore_wait(barrier, greeted)
            signal(diag_sem, nearby(1, core))

        exchange(c, 1)[1].start()

        if c == 2:
            exchange(c, 3)[1].start()

        exchange(c, 2)[1].start()
        mine, remote, local = exchange(c, 0)

        @pl.when(mine)
        def _():
            local.start()

        @pl.when(jnp.logical_not(mine))
        def _():
            remote.start()

        if c == 1:
            pl.semaphore_wait(diag_sem, 1)
            exchange(0, 3)[1].start()
            exchange(1, 3)[1].start()

    for copy in const_copies:
        copy.wait()

    def landed(s, c):
        pltpu.make_async_copy(sbuf.at[0, rows(c), :], rbuf.at[s, rows(c), :], recv_sem.at[s, c]).wait()

    def hand_on(c):
        return pltpu.make_async_remote_copy(
            src_ref=rbuf.at[0, rows(c), :], dst_ref=rbuf.at[SLOTS, rows(c), :], send_sem=pass_sem.at[c],
            recv_sem=recv_sem.at[SLOTS, c], device_id=(device(quad - 1, chip),), device_id_type=MESH)

    bins = LAGS
    half = bins // 2

    def position(s, c, off):
        u = rbuf[s, row0(c):row0(c) + frames, :]
        return u * box[c] + off

    def total(s, c):
        return rbuf[s, frames + c:frames + c + 1, :]

    def transform(x):
        hi, lo = split(x)
        return jnp.dot(fwd[...], jnp.concatenate([hi, lo, hi], axis=0), preferred_element_type=F32)

    offs = {}

    def arrive(c):
        landed(0, c)

        @pl.when(quad > 0)
        def _():
            hand_on(c).start()

        for s in range(1, SLOTS):
            landed(s, c)

    def main(c):
        mid = rbuf[2, row0(c):row0(c) + frames, :]
        ref = jnp.sum(mid, axis=0, keepdims=True) * (-1.0 / frames)
        shift = [ref - total(1, c) - total(0, c), ref - total(1, c), ref, ref + total(2, c)]
        offs[c] = (ref + total(2, c) + total(3, c)) * box[c]
        xs = [position(s, c, shift[s] * box[c]) for s in range(SLOTS)]
        squares = [x * x for x in xs]
        all_sq = (squares[0] + squares[1]) + (squares[2] + squares[3])
        if c == 0:
            first_sq[...] = squares[0]
            last_sq[...] = squares[3]
            sum_sq[...] = all_sq
        else:
            first_sq[...] = first_sq[...] + squares[0]
            last_sq[...] = last_sq[...] + squares[3]
            sum_sq[...] = sum_sq[...] + all_sq
        for s in range(SLOTS):
            spec[c, s] = transform(xs[s])
        for sign, base in ((1, 0), (-1, half)):
            @pl.loop(0, half // SUB)
            def _(r):
                re_rows = pl.ds(pl.multiple_of(base + r * SUB, SUB), SUB)
                im_rows = pl.ds(pl.multiple_of(bins + base + r * SUB, SUB), SUB)
                res = [spec[c, s, re_rows, :] for s in range(SLOTS)]
                ims = [spec[c, s, im_rows, :] for s in range(SLOTS)]
                z_re = z_im = None
                for s in range(SLOTS):
                    if s < SLOTS - 1:
                        y_re = res[s] + ims[s + 1] if sign > 0 else res[s] - ims[s + 1]
                        y_im = ims[s] - res[s + 1] if sign > 0 else ims[s] + res[s + 1]
                        p_re = res[s] * y_re + ims[s] * y_im
                        p_im = res[s] * y_im - ims[s] * y_re
                        z_im = p_im if z_im is None else z_im + p_im
                    else:
                        p_re = res[s] * res[s] + ims[s] * ims[s]
                    z_re = p_re if z_re is None else z_re + p_re
                if c == 0:
                    zbuf[re_rows, :] = z_re
                    zbuf[im_rows, :] = z_im
                else:
                    zbuf[re_rows, :] = zbuf[re_rows, :] + z_re
                    zbuf[im_rows, :] = zbuf[im_rows, :] + z_im

    def halo(c):
        off = offs[c]

        @pl.when(jnp.logical_not(is_last))
        def _():
            landed(SLOTS, c)
            x = position(SLOTS, c, off)
            if c == 0:
                halo_sq[...] = x * x
            else:
                halo_sq[...] = halo_sq[...] + x * x
            spec[c, 0] = transform(x)
            for sign, base in ((1, 0), (-1, half)):
                @pl.loop(0, half // SUB)
                def _(r):
                    re_rows = pl.ds(pl.multiple_of(base + r * SUB, SUB), SUB)
                    im_rows = pl.ds(pl.multiple_of(bins + base + r * SUB, SUB), SUB)
                    x_re, x_im = spec[c, SLOTS - 1, re_rows, :], spec[c, SLOTS - 1, im_rows, :]
                    y_re, y_im = spec[c, 0, im_rows, :], spec[c, 0, re_rows, :]
                    if sign > 0:
                        zbuf[re_rows, :] = zbuf[re_rows, :] + (x_re * y_re - x_im * y_im)
                        zbuf[im_rows, :] = zbuf[im_rows, :] - (x_re * y_im + x_im * y_re)
                    else:
                        zbuf[re_rows, :] = zbuf[re_rows, :] - (x_re * y_re - x_im * y_im)
                        zbuf[im_rows, :] = zbuf[im_rows, :] + (x_re * y_im + x_im * y_re)

    @pl.when(is_last)
    def _():
        halo_sq[...] = jnp.zeros_like(halo_sq)

    arrive(0)
    spread(0, rounds)
    arrive(1)
    main(0)
    main(1)
    halo(0)
    arrive(2)
    main(2)
    halo(1)
    halo(2)

    z_hi, z_lo = split(zbuf[...])
    w_hi, w_lo = split(halo_sq[...] - first_sq[...])
    v_hi, v_lo = split(jnp.where(is_last, -last_sq[...], 0.0))
    lag_sum = jnp.dot(inv[...], jnp.concatenate([z_hi, z_lo, z_hi, w_hi, w_lo, v_hi, v_lo], axis=0),
                      preferred_element_type=F32)
    lag_sum = lag_sum + 2.0 * jnp.sum(sum_sq[...], axis=0, keepdims=True)
    by_atom = lag_sum.T
    for g in range(SLOTS):
        for p in range(sub_planes):
            for k in range(2):
                first = p * SLOTS * width + g * width + k * per_owner
                tbuf[2 * (g * sub_planes + p) + k] = by_atom[first:first + per_owner, :]

    @pl.loop(0, quads)
    def _(q):
        @pl.when(q != quad)
        def _():
            pltpu.make_async_remote_copy(
                src_ref=tbuf.at[q], dst_ref=part.at[quad], send_sem=part_send, recv_sem=part_recv,
                device_id=(device(q, chip),), device_id_type=MESH).start()

    part[quad] = tbuf[quad]
    others = pl.ds(0, quads - 1)
    pltpu.make_async_remote_copy(
        src_ref=tbuf.at[others], dst_ref=part.at[others], send_sem=part_send, recv_sem=part_recv,
        device_id=((me + 1) % n,), device_id_type=MESH).wait()
    out[...] = jnp.sum(part[...], axis=0)

    for c in range(dims):
        for o in (3, 1, 2):
            exchange(c, o)[1].wait_send()
        mine, remote, local = exchange(c, 0)

        @pl.when(jnp.logical_not(mine))
        def _():
            remote.wait_send()

        @pl.when(quad > 0)
        def _():
            hand_on(c).wait_send()


def tables(frames):
    f = np.concatenate([np.arange(0, LAGS, 2), np.arange(1, LAGS, 2)]) + 0.5
    t = np.arange(frames)
    angle = 2.0 * np.pi * f[:, None] * t[None, :] / (2 * LAGS)
    fwd = np.concatenate([np.cos(angle), -np.sin(angle)], axis=0).astype(np.float32)
    back = (2.0 * np.pi * f[None, :] * np.arange(LAGS)[:, None]) / (2 * LAGS)
    inv = np.concatenate([np.cos(back), -np.sin(back)], axis=1) * (-2.0 / LAGS)
    inv = inv.astype(np.float32)

    def halves(x):
        hi = x.astype(jnp.bfloat16)
        return hi, (x - hi.astype(np.float32)).astype(jnp.bfloat16)

    k = np.arange(LAGS)[:, None]
    low = (t[None, :] < k).astype(jnp.bfloat16)
    high = (t[None, :] >= frames - k).astype(jnp.bfloat16)
    f_hi, f_lo = halves(fwd)
    i_hi, i_lo = halves(inv)
    return (np.concatenate([f_hi, f_hi, f_lo], axis=1),
            np.concatenate([i_hi, i_hi, i_lo, low, low, high, high], axis=1))


def on_device(n, wrapped, crossings, box_size):
    frames, dims, atoms = wrapped.shape
    per_owner = atoms // n
    quads = n // SLOTS
    assert frames == LAGS and atoms == SLOTS * LANES and n % GROUP == 0 and LANES % (GROUP * per_owner) == 0
    fwd, inv = tables(frames)
    any_spec = pl.BlockSpec(memory_space=pltpu.HBM)
    piece = SUB + dims * frames
    lag_sum = pl.pallas_call(
        functools.partial(kernel, n),
        out_shape=jax.ShapeDtypeStruct((per_owner, LAGS), F32),
        in_specs=[any_spec] * 5,
        out_specs=pl.BlockSpec(memory_space=pltpu.VMEM),
        scratch_shapes=[
            pltpu.VMEM((dims, frames, atoms), F32),
            pltpu.VMEM((dims, frames, atoms), jnp.int32),
            pltpu.VMEM((SLOTS, piece, LANES), F32),
            pltpu.VMEM((SLOTS + 1, piece, LANES), F32),
            pltpu.VMEM(fwd.shape, BF16),
            pltpu.VMEM(inv.shape, BF16),
            pltpu.VMEM((dims, SLOTS, 2 * LAGS, LANES), F32),
            pltpu.VMEM((2 * LAGS, LANES), F32),
            pltpu.VMEM((frames, LANES), F32),
            pltpu.VMEM((frames, LANES), F32),
            pltpu.VMEM((frames, LANES), F32),
            pltpu.VMEM((frames, LANES), F32),
            pltpu.VMEM((quads, per_owner, LAGS), F32),
            pltpu.VMEM((quads, per_owner, LAGS), F32),
            pltpu.SemaphoreType.DMA((dims, 2)),
            pltpu.SemaphoreType.DMA((3,)),
            pltpu.SMEM((dims,), F32),
            pltpu.SemaphoreType.DMA((SLOTS, dims)),
            pltpu.SemaphoreType.DMA((SLOTS + 1, dims)),
            pltpu.SemaphoreType.DMA((dims,)),
            pltpu.SemaphoreType.DMA,
            pltpu.SemaphoreType.DMA,
            pltpu.SemaphoreType.REGULAR,
            pltpu.SemaphoreType.REGULAR,
            pltpu.SemaphoreType.REGULAR,
        ],
        compiler_params=pltpu.CompilerParams(collective_id=0, has_side_effects=True, vmem_limit_bytes=55200*1024),
    )(jnp.transpose(wrapped, (1, 0, 2)), jnp.transpose(crossings, (1, 0, 2)), box_size,
      jnp.asarray(fwd), jnp.asarray(inv))
    divisor = (n * frames - jnp.arange(LAGS, dtype=jnp.int32)).astype(F32)
    return lag_sum / divisor[None, :]


def solution(mesh):
    in_specs = (P("tm", None, None), P("tm", None, None), P())
    out_specs = P("tm", None)
    return jax.shard_map(
        functools.partial(on_device, mesh.shape["tm"]), mesh=mesh,
        in_specs=in_specs, out_specs=out_specs, check_vma=False)
```

```python
import functools

import jax
import jax.numpy as jnp
import numpy as np
from jax import lax
from jax.experimental import pallas as pl
from jax.experimental.pallas import tpu as pltpu
from jax.sharding import PartitionSpec as P

LAGS = 128
LANES = 128
SUB = 8
SLOTS = 4
GROUP = 2 * SLOTS
MESH = pl.DeviceIdType.MESH
F32 = jnp.float32
BF16 = jnp.bfloat16


def split(x):
    hi = x.astype(BF16)
    return hi, (x - hi.astype(F32)).astype(BF16)


def kernel(n, wrapped, crossings, box_hbm, fwd_hbm, inv_hbm, out, wbuf, xbuf, sbuf, rbuf, fwd, inv, spec, zbuf,
           first_sq, last_sq, halo_sq, sum_sq, tbuf, part, load_sem, const_sem, box, send_sem, recv_sem, pass_sem,
           part_send, part_recv, diag_sem, up_sem, down_sem):
    dims, frames = wbuf.shape[:2]
    per_owner = out.shape[0]
    planes = n // GROUP
    quads = n // SLOTS
    width = 2 * per_owner
    sub_planes = LANES // (SLOTS * width)
    me = lax.axis_index("tm")
    plane = me // GROUP
    j = me % GROUP
    chip, core = j // 2, j % 2
    quad = 2 * plane + core
    slot = j % SLOTS
    is_last = quad == quads - 1

    def device(q, i):
        return GROUP * (q // 2) + 2 * i + q % 2

    x, y = chip % 2, chip // 2
    partner = me + 1 - 2 * core

    def nearby(o, k):
        return GROUP * plane + 2 * (2 * ((y + o // 2) % 2) + (x + o) % 2) + k

    def signal(sem, dst):
        pl.semaphore_signal(sem, inc=1, device_id=(dst,), device_id_type=MESH)

    barrier = pltpu.get_barrier_semaphore()
    below, above = plane > 0, plane < planes - 1
    signal(barrier, partner)
    for k in range(2):
        signal(barrier, nearby(1, k))
        signal(barrier, nearby(2, k))

    @pl.when(below)
    def _():
        for k in range(2):
            signal(barrier, GROUP * (plane - 1) + 2 * chip + k)

    @pl.when(above)
    def _():
        for k in range(2):
            signal(barrier, GROUP * (plane + 1) + 2 * chip + k)

    greeted = 5 + 2 * jnp.where(below, 1, 0) + 2 * jnp.where(above, 1, 0)

    def spread(first, last):
        @pl.loop(first, last)
        def _(r):
            @pl.when(below)
            def _():
                signal(up_sem, me - GROUP)

            @pl.when(above)
            def _():
                signal(down_sem, me + GROUP)

            @pl.when(above)
            def _():
                pl.semaphore_wait(up_sem, 1)

            @pl.when(below)
            def _():
                pl.semaphore_wait(down_sem, 1)

    rounds = max(planes - 2, 0)

    def load(c, which):
        src, dst = ((wrapped, wbuf), (crossings, xbuf))[which]
        return pltpu.make_async_copy(src.at[c], dst.at[c], load_sem.at[c, which])

    load(0, 1).start()
    load(0, 0).start()
    for c in range(1, dims):
        load(c, 1).start()
    for c in range(1, dims):
        load(c, 0).start()
    const_copies = [pltpu.make_async_copy(fwd_hbm, fwd, const_sem.at[0]),
                    pltpu.make_async_copy(inv_hbm, inv, const_sem.at[1]),
                    pltpu.make_async_copy(box_hbm, box, const_sem.at[2])]
    for copy in const_copies:
        copy.start()

    lane = lax.broadcasted_iota(jnp.int32, (SUB, LANES), 1)
    sub = lax.broadcasted_iota(jnp.int32, (SUB, LANES), 0)

    def swap(a, b, dist):
        low = (lane[0:1] & dist) == 0
        return (jnp.where(low, a, pltpu.roll(b, dist, 1)), jnp.where(low, pltpu.roll(a, LANES - dist, 1), b))

    def pack(groups):
        a = list(groups)
        for k in (0, 1):
            a[k], a[k + 2] = swap(a[k], a[k + 2], 2 * width)
        for k in (0, 2):
            a[k], a[k + 1] = swap(a[k], a[k + 1], width)
        return a

    ones = jnp.ones((SUB, frames), BF16)
    tri = (lax.broadcasted_iota(jnp.int32, (frames, frames), 1)
           <= lax.broadcasted_iota(jnp.int32, (frames, frames), 0)).astype(F32).astype(BF16)

    def rows(c):
        return (pl.ds(0, frames), pl.ds(frames, SUB + frames), pl.ds(SUB + 2 * frames, frames))[c]

    def row0(c):
        return c * frames + (SUB if c > 0 else 0)

    def lanes(g):
        return pl.ds(g * LANES, LANES)

    own_quad = 2 * plane + j // SLOTS

    def exchange(c, o):
        i = 2 * ((chip // 2 + o // 2) % 2) + (chip + o) % 2
        dst = device(own_quad, i)
        src, to = sbuf.at[i, rows(c), :], rbuf.at[slot, rows(c), :]
        remote = pltpu.make_async_remote_copy(
            src_ref=src, dst_ref=to, send_sem=send_sem.at[o, c], recv_sem=recv_sem.at[slot, c],
            device_id=(dst,), device_id_type=MESH)
        return dst == me, remote, pltpu.make_async_copy(src, to, recv_sem.at[slot, c])

    for c in range(dims):
        if c == 1:
            for k in range(1, dims):
                load(k, 1).wait()
            totals = [jnp.dot(ones, xbuf[c].astype(F32).astype(BF16), preferred_element_type=F32) for c in range(dims)]
            groups = []
            for g in range(SLOTS):
                t = [v[:, g * LANES:(g + 1) * LANES] for v in totals]
                groups.append(jnp.where(sub == 0, t[0], jnp.where(sub == 1, t[1], t[2])))
            for i, v in enumerate(pack(groups)):
                sbuf[i, frames:frames + SUB, :] = v
        if c == 0:
            load(c, 1).wait()
        load(c, 0).wait()
        counts = jnp.dot(tri, xbuf[c].astype(F32).astype(BF16), preferred_element_type=F32)
        wbuf[c] = wbuf[c] + counts
        for r in range(0, frames, SUB):
            for i, v in enumerate(pack([wbuf[c, r:r + SUB, lanes(g)] for g in range(SLOTS)])):
                sbuf[i, row0(c) + r:row0(c) + r + SUB, :] = v
        if c == 0:
            pl.semaphore_wait(barrier, greeted)
            signal(diag_sem, nearby(1, core))

        exchange(c, 1)[1].start()

        if c == 2:
            exchange(c, 3)[1].start()

        exchange(c, 2)[1].start()
        mine, remote, local = exchange(c, 0)

        @pl.when(mine)
        def _():
            local.start()

        @pl.when(jnp.logical_not(mine))
        def _():
            remote.start()

        if c == 1:
            pl.semaphore_wait(diag_sem, 1)
            exchange(0, 3)[1].start()
            exchange(1, 3)[1].start()

    for copy in const_copies:
        copy.wait()

    def landed(s, c):
        pltpu.make_async_copy(sbuf.at[0, rows(c), :], rbuf.at[s, rows(c), :], recv_sem.at[s, c]).wait()

    def hand_on(c):
        return pltpu.make_async_remote_copy(
            src_ref=rbuf.at[0, rows(c), :], dst_ref=rbuf.at[SLOTS, rows(c), :], send_sem=pass_sem.at[c],
            recv_sem=recv_sem.at[SLOTS, c], device_id=(device(quad - 1, chip),), device_id_type=MESH)

    bins = LAGS
    half = bins // 2

    def position(s, c, off):
        u = rbuf[s, row0(c):row0(c) + frames, :]
        return u * box[c] + off

    def total(s, c):
        return rbuf[s, frames + c:frames + c + 1, :]

    def transform(x):
        hi, lo = split(x)
        return jnp.dot(fwd[...], jnp.concatenate([hi, lo, hi], axis=0), preferred_element_type=F32)

    offs = {}

    def arrive(c):
        landed(0, c)

        @pl.when(quad > 0)
        def _():
            hand_on(c).start()

        for s in range(1, SLOTS):
            landed(s, c)

    def main(c):
        mid = rbuf[2, row0(c):row0(c) + frames, :]
        ref = jnp.sum(mid, axis=0, keepdims=True) * (-1.0 / frames)
        shift = [ref - total(1, c) - total(0, c), ref - total(1, c), ref, ref + total(2, c)]
        offs[c] = (ref + total(2, c) + total(3, c)) * box[c]
        xs = [position(s, c, shift[s] * box[c]) for s in range(SLOTS)]
        squares = [x * x for x in xs]
        all_sq = (squares[0] + squares[1]) + (squares[2] + squares[3])
        if c == 0:
            first_sq[...] = squares[0]
            last_sq[...] = squares[3]
            sum_sq[...] = all_sq
        else:
            first_sq[...] = first_sq[...] + squares[0]
            last_sq[...] = last_sq[...] + squares[3]
            sum_sq[...] = sum_sq[...] + all_sq
        for s in range(SLOTS):
            spec[c, s] = transform(xs[s])
        for sign, base in ((1, 0), (-1, half)):
            @pl.loop(0, half // SUB)
            def _(r):
                re_rows = pl.ds(pl.multiple_of(base + r * SUB, SUB), SUB)
                im_rows = pl.ds(pl.multiple_of(bins + base + r * SUB, SUB), SUB)
                res = [spec[c, s, re_rows, :] for s in range(SLOTS)]
                ims = [spec[c, s, im_rows, :] for s in range(SLOTS)]
                z_re = z_im = None
                for s in range(SLOTS):
                    if s < SLOTS - 1:
                        y_re = res[s] + ims[s + 1] if sign > 0 else res[s] - ims[s + 1]
                        y_im = ims[s] - res[s + 1] if sign > 0 else ims[s] + res[s + 1]
                        p_re = res[s] * y_re + ims[s] * y_im
                        p_im = res[s] * y_im - ims[s] * y_re
                        z_im = p_im if z_im is None else z_im + p_im
                    else:
                        p_re = res[s] * res[s] + ims[s] * ims[s]
                    z_re = p_re if z_re is None else z_re + p_re
                if c == 0:
                    zbuf[re_rows, :] = z_re
                    zbuf[im_rows, :] = z_im
                else:
                    zbuf[re_rows, :] = zbuf[re_rows, :] + z_re
                    zbuf[im_rows, :] = zbuf[im_rows, :] + z_im

    def halo(c):
        off = offs[c]

        @pl.when(jnp.logical_not(is_last))
        def _():
            landed(SLOTS, c)
            x = position(SLOTS, c, off)
            if c == 0:
                halo_sq[...] = x * x
            else:
                halo_sq[...] = halo_sq[...] + x * x
            spec[c, 0] = transform(x)
            for sign, base in ((1, 0), (-1, half)):
                @pl.loop(0, half // SUB)
                def _(r):
                    re_rows = pl.ds(pl.multiple_of(base + r * SUB, SUB), SUB)
                    im_rows = pl.ds(pl.multiple_of(bins + base + r * SUB, SUB), SUB)
                    x_re, x_im = spec[c, SLOTS - 1, re_rows, :], spec[c, SLOTS - 1, im_rows, :]
                    y_re, y_im = spec[c, 0, im_rows, :], spec[c, 0, re_rows, :]
                    if sign > 0:
                        zbuf[re_rows, :] = zbuf[re_rows, :] + (x_re * y_re - x_im * y_im)
                        zbuf[im_rows, :] = zbuf[im_rows, :] - (x_re * y_im + x_im * y_re)
                    else:
                        zbuf[re_rows, :] = zbuf[re_rows, :] - (x_re * y_re - x_im * y_im)
                        zbuf[im_rows, :] = zbuf[im_rows, :] + (x_re * y_im + x_im * y_re)

    @pl.when(is_last)
    def _():
        halo_sq[...] = jnp.zeros_like(halo_sq)

    arrive(0)
    spread(0, rounds)
    arrive(1)
    main(0)
    main(1)
    halo(0)
    arrive(2)
    main(2)
    halo(1)
    halo(2)

    z_hi, z_lo = split(zbuf[...])
    w_hi, w_lo = split(halo_sq[...] - first_sq[...])
    v_hi, v_lo = split(jnp.where(is_last, -last_sq[...], 0.0))
    lag_sum = jnp.dot(inv[...], jnp.concatenate([z_hi, z_lo, z_hi, w_hi, w_lo, v_hi, v_lo], axis=0),
                      preferred_element_type=F32)
    lag_sum = lag_sum + 2.0 * jnp.sum(sum_sq[...], axis=0, keepdims=True)
    by_atom = lag_sum.T
    for g in range(SLOTS):
        for p in range(sub_planes):
            for k in range(2):
                first = p * SLOTS * width + g * width + k * per_owner
                tbuf[2 * (g * sub_planes + p) + k] = by_atom[first:first + per_owner, :]

    @pl.loop(0, quads)
    def _(q):
        @pl.when(q != quad)
        def _():
            pltpu.make_async_remote_copy(
                src_ref=tbuf.at[q], dst_ref=part.at[quad], send_sem=part_send, recv_sem=part_recv,
                device_id=(device(q, chip),), device_id_type=MESH).start()

    part[quad] = tbuf[quad]
    others = pl.ds(0, quads - 1)
    pltpu.make_async_remote_copy(
        src_ref=tbuf.at[others], dst_ref=part.at[others], send_sem=part_send, recv_sem=part_recv,
        device_id=((me + 1) % n,), device_id_type=MESH).wait()
    out[...] = jnp.sum(part[...], axis=0)

    for c in range(dims):
        for o in (3, 1, 2):
            exchange(c, o)[1].wait_send()
        mine, remote, local = exchange(c, 0)

        @pl.when(jnp.logical_not(mine))
        def _():
            remote.wait_send()

        @pl.when(quad > 0)
        def _():
            hand_on(c).wait_send()


def tables(frames):
    f = np.concatenate([np.arange(0, LAGS, 2), np.arange(1, LAGS, 2)]) + 0.5
    t = np.arange(frames)
    angle = 2.0 * np.pi * f[:, None] * t[None, :] / (2 * LAGS)
    fwd = np.concatenate([np.cos(angle), -np.sin(angle)], axis=0).astype(np.float32)
    back = (2.0 * np.pi * f[None, :] * np.arange(LAGS)[:, None]) / (2 * LAGS)
    inv = np.concatenate([np.cos(back), -np.sin(back)], axis=1) * (-2.0 / LAGS)
    inv = inv.astype(np.float32)

    def halves(x):
        hi = x.astype(jnp.bfloat16)
        return hi, (x - hi.astype(np.float32)).astype(jnp.bfloat16)

    k = np.arange(LAGS)[:, None]
    low = (t[None, :] < k).astype(jnp.bfloat16)
    high = (t[None, :] >= frames - k).astype(jnp.bfloat16)
    f_hi, f_lo = halves(fwd)
    i_hi, i_lo = halves(inv)
    return (np.concatenate([f_hi, f_hi, f_lo], axis=1),
            np.concatenate([i_hi, i_hi, i_lo, low, low, high, high], axis=1))


def on_device(n, wrapped, crossings, box_size):
    frames, dims, atoms = wrapped.shape
    per_owner = atoms // n
    quads = n // SLOTS
    assert frames == LAGS and atoms == SLOTS * LANES and n % GROUP == 0 and LANES % (GROUP * per_owner) == 0
    fwd, inv = tables(frames)
    any_spec = pl.BlockSpec(memory_space=pltpu.HBM)
    piece = SUB + dims * frames
    lag_sum = pl.pallas_call(
        functools.partial(kernel, n),
        out_shape=jax.ShapeDtypeStruct((per_owner, LAGS), F32),
        in_specs=[any_spec] * 5,
        out_specs=pl.BlockSpec(memory_space=pltpu.VMEM),
        scratch_shapes=[
            pltpu.VMEM((dims, frames, atoms), F32),
            pltpu.VMEM((dims, frames, atoms), jnp.int32),
            pltpu.VMEM((SLOTS, piece, LANES), F32),
            pltpu.VMEM((SLOTS + 1, piece, LANES), F32),
            pltpu.VMEM(fwd.shape, BF16),
            pltpu.VMEM(inv.shape, BF16),
            pltpu.VMEM((dims, SLOTS, 2 * LAGS, LANES), F32),
            pltpu.VMEM((2 * LAGS, LANES), F32),
            pltpu.VMEM((frames, LANES), F32),
            pltpu.VMEM((frames, LANES), F32),
            pltpu.VMEM((frames, LANES), F32),
            pltpu.VMEM((frames, LANES), F32),
            pltpu.VMEM((quads, per_owner, LAGS), F32),
            pltpu.VMEM((quads, per_owner, LAGS), F32),
            pltpu.SemaphoreType.DMA((dims, 2)),
            pltpu.SemaphoreType.DMA((3,)),
            pltpu.SMEM((dims,), F32),
            pltpu.SemaphoreType.DMA((SLOTS, dims)),
            pltpu.SemaphoreType.DMA((SLOTS + 1, dims)),
            pltpu.SemaphoreType.DMA((dims,)),
            pltpu.SemaphoreType.DMA,
            pltpu.SemaphoreType.DMA,
            pltpu.SemaphoreType.REGULAR,
            pltpu.SemaphoreType.REGULAR,
            pltpu.SemaphoreType.REGULAR,
        ],
        compiler_params=pltpu.CompilerParams(collective_id=0, has_side_effects=True, vmem_limit_bytes=32 * 2**20),
    )(*(pltpu.with_memory_space_constraint(v, pltpu.HBM) for v in (
        jnp.transpose(wrapped, (1, 0, 2)), jnp.transpose(crossings, (1, 0, 2)), box_size,
        jnp.asarray(fwd), jnp.asarray(inv))))
    divisor = (n * frames - jnp.arange(LAGS, dtype=jnp.int32)).astype(F32)
    return lag_sum / divisor[None, :]


def solution(mesh):
    in_specs = (P("tm", None, None), P("tm", None, None), P())
    out_specs = P("tm", None)
    return jax.shard_map(
        functools.partial(on_device, mesh.shape["tm"]), mesh=mesh,
        in_specs=in_specs, out_specs=out_specs, check_vma=False)
```

```python
import functools

import jax
import jax.numpy as jnp
import numpy as np
from jax import lax
from jax.experimental import pallas as pl
from jax.experimental.pallas import tpu as pltpu
from jax.sharding import PartitionSpec as P

LAGS = 128
LANES = 128
SUB = 8
SLOTS = 4
GROUP = 2 * SLOTS
MESH = pl.DeviceIdType.MESH
F32 = jnp.float32
BF16 = jnp.bfloat16


def split(x):
    hi = x.astype(BF16)
    return hi, (x - hi.astype(F32)).astype(BF16)


def kernel(n, wrapped, crossings, box_hbm, fwd_hbm, inv_hbm, out, wbuf, xbuf, sbuf, rbuf, fwd, inv, spec, zbuf,
           first_sq, last_sq, halo_sq, sum_sq, tbuf, part, load_sem, const_sem, box, send_sem, recv_sem, pass_sem,
           part_send, part_recv, diag_sem, up_sem, down_sem):
    dims, frames = wbuf.shape[:2]
    per_owner = out.shape[0]
    planes = n // GROUP
    quads = n // SLOTS
    width = 2 * per_owner
    sub_planes = LANES // (SLOTS * width)
    me = lax.axis_index("tm")
    plane = me // GROUP
    j = me % GROUP
    chip, core = j // 2, j % 2
    quad = 2 * plane + core
    slot = j % SLOTS
    is_last = quad == quads - 1

    def device(q, i):
        return GROUP * (q // 2) + 2 * i + q % 2

    x, y = chip % 2, chip // 2
    partner = me + 1 - 2 * core

    def nearby(o, k):
        return GROUP * plane + 2 * (2 * ((y + o // 2) % 2) + (x + o) % 2) + k

    def signal(sem, dst):
        pl.semaphore_signal(sem, inc=1, device_id=(dst,), device_id_type=MESH)

    barrier = pltpu.get_barrier_semaphore()
    below, above = plane > 0, plane < planes - 1
    signal(barrier, partner)
    for k in range(2):
        signal(barrier, nearby(1, k))
        signal(barrier, nearby(2, k))

    @pl.when(below)
    def _():
        for k in range(2):
            signal(barrier, GROUP * (plane - 1) + 2 * chip + k)

    @pl.when(above)
    def _():
        for k in range(2):
            signal(barrier, GROUP * (plane + 1) + 2 * chip + k)

    greeted = 5 + 2 * jnp.where(below, 1, 0) + 2 * jnp.where(above, 1, 0)

    def spread(first, last):
        @pl.loop(first, last)
        def _(r):
            @pl.when(below)
            def _():
                signal(up_sem, me - GROUP)

            @pl.when(above)
            def _():
                signal(down_sem, me + GROUP)

            @pl.when(above)
            def _():
                pl.semaphore_wait(up_sem, 1)

            @pl.when(below)
            def _():
                pl.semaphore_wait(down_sem, 1)

    rounds = max(planes - 2, 0)

    def load(c, which):
        src, dst = ((wrapped, wbuf), (crossings, xbuf))[which]
        return pltpu.make_async_copy(src.at[c], dst.at[c], load_sem.at[c, which])

    load(0, 1).start()
    load(0, 0).start()
    for c in range(1, dims):
        load(c, 1).start()
    for c in range(1, dims):
        load(c, 0).start()
    const_copies = [pltpu.make_async_copy(fwd_hbm, fwd, const_sem.at[0]),
                    pltpu.make_async_copy(inv_hbm, inv, const_sem.at[1]),
                    pltpu.make_async_copy(box_hbm, box, const_sem.at[2])]

    lane = lax.broadcasted_iota(jnp.int32, (SUB, LANES), 1)
    sub = lax.broadcasted_iota(jnp.int32, (SUB, LANES), 0)

    def swap(a, b, dist):
        low = (lane[0:1] & dist) == 0
        return (jnp.where(low, a, pltpu.roll(b, dist, 1)), jnp.where(low, pltpu.roll(a, LANES - dist, 1), b))

    def pack(groups):
        a = list(groups)
        for k in (0, 1):
            a[k], a[k + 2] = swap(a[k], a[k + 2], 2 * width)
        for k in (0, 2):
            a[k], a[k + 1] = swap(a[k], a[k + 1], width)
        return a

    ones = jnp.ones((SUB, frames), BF16)
    tri = (lax.broadcasted_iota(jnp.int32, (frames, frames), 1)
           <= lax.broadcasted_iota(jnp.int32, (frames, frames), 0)).astype(F32).astype(BF16)

    def rows(c):
        return (pl.ds(0, frames), pl.ds(frames, SUB + frames), pl.ds(SUB + 2 * frames, frames))[c]

    def row0(c):
        return c * frames + (SUB if c > 0 else 0)

    def lanes(g):
        return pl.ds(g * LANES, LANES)

    own_quad = 2 * plane + j // SLOTS

    def exchange(c, o):
        i = 2 * ((chip // 2 + o // 2) % 2) + (chip + o) % 2
        dst = device(own_quad, i)
        src, to = sbuf.at[i, rows(c), :], rbuf.at[slot, rows(c), :]
        remote = pltpu.make_async_remote_copy(
            src_ref=src, dst_ref=to, send_sem=send_sem.at[o, c], recv_sem=recv_sem.at[slot, c],
            device_id=(dst,), device_id_type=MESH)
        return dst == me, remote, pltpu.make_async_copy(src, to, recv_sem.at[slot, c])

    for c in range(dims):
        if c == 1:
            for k in range(1, dims):
                load(k, 1).wait()
            totals = [jnp.dot(ones, xbuf[c].astype(F32).astype(BF16), preferred_element_type=F32) for c in range(dims)]
            groups = []
            for g in range(SLOTS):
                t = [v[:, g * LANES:(g + 1) * LANES] for v in totals]
                groups.append(jnp.where(sub == 0, t[0], jnp.where(sub == 1, t[1], t[2])))
            for i, v in enumerate(pack(groups)):
                sbuf[i, frames:frames + SUB, :] = v
        if c == 0:
            load(c, 1).wait()
        load(c, 0).wait()
        counts = jnp.dot(tri, xbuf[c].astype(F32).astype(BF16), preferred_element_type=F32)
        wbuf[c] = wbuf[c] + counts
        for r in range(0, frames, SUB):
            for i, v in enumerate(pack([wbuf[c, r:r + SUB, lanes(g)] for g in range(SLOTS)])):
                sbuf[i, row0(c) + r:row0(c) + r + SUB, :] = v
        if c == 0:
            pl.semaphore_wait(barrier, greeted)
            signal(diag_sem, nearby(1, core))

        if c < 2:
            exchange(c, 1)[1].start()
        else:
            @pl.when(chip == SLOTS - 1)
            def _():
                exchange(2, 3)[1].start()
                exchange(2, 1)[1].start()

            @pl.when(chip != SLOTS - 1)
            def _():
                exchange(2, 1)[1].start()
                exchange(2, 3)[1].start()

        exchange(c, 2)[1].start()
        mine, remote, local = exchange(c, 0)

        @pl.when(mine)
        def _():
            local.start()

        @pl.when(jnp.logical_not(mine))
        def _():
            remote.start()

        if c == 0:
            for copy in const_copies:
                copy.start()
        if c == 1:
            pl.semaphore_wait(diag_sem, 1)
            exchange(0, 3)[1].start()
            exchange(1, 3)[1].start()

    for copy in const_copies:
        copy.wait()

    def landed(s, c):
        pltpu.make_async_copy(sbuf.at[0, rows(c), :], rbuf.at[s, rows(c), :], recv_sem.at[s, c]).wait()

    def hand_on(c):
        return pltpu.make_async_remote_copy(
            src_ref=rbuf.at[0, rows(c), :], dst_ref=rbuf.at[SLOTS, rows(c), :], send_sem=pass_sem.at[c],
            recv_sem=recv_sem.at[SLOTS, c], device_id=(device(quad - 1, chip),), device_id_type=MESH)

    bins = LAGS
    half = bins // 2

    def position(s, c, off):
        u = rbuf[s, row0(c):row0(c) + frames, :]
        return u * box[c] + off

    def total(s, c):
        return rbuf[s, frames + c:frames + c + 1, :]

    def transform(x):
        hi, lo = split(x)
        return jnp.dot(fwd[...], jnp.concatenate([hi, lo, hi], axis=0), preferred_element_type=F32)

    offs = {}

    direct = jnp.logical_and(x == 0, y == 1)

    def take_first(c):
        landed(0, c)

        @pl.when(quad > 0)
        def _():
            hand_on(c).start()

    def arrive(c):
        @pl.when(jnp.logical_not(direct))
        def _():
            take_first(c)

        for s in range(1, SLOTS):
            landed(s, c)

    def main(c):
        mid = rbuf[2, row0(c):row0(c) + frames, :]
        ref = jnp.sum(mid, axis=0, keepdims=True) * (-1.0 / frames)
        shift = [ref - total(1, c) - total(0, c), ref - total(1, c), ref, ref + total(2, c)]
        offs[c] = (ref + total(2, c) + total(3, c)) * box[c]
        xs = [position(s, c, shift[s] * box[c]) for s in range(SLOTS)]
        squares = [x * x for x in xs]
        all_sq = (squares[0] + squares[1]) + (squares[2] + squares[3])
        if c == 0:
            first_sq[...] = squares[0]
            last_sq[...] = squares[3]
            sum_sq[...] = all_sq
        else:
            first_sq[...] = first_sq[...] + squares[0]
            last_sq[...] = last_sq[...] + squares[3]
            sum_sq[...] = sum_sq[...] + all_sq
        for s in range(SLOTS):
            spec[c, s] = transform(xs[s])
        for sign, base in ((1, 0), (-1, half)):
            @pl.loop(0, half // SUB)
            def _(r):
                re_rows = pl.ds(pl.multiple_of(base + r * SUB, SUB), SUB)
                im_rows = pl.ds(pl.multiple_of(bins + base + r * SUB, SUB), SUB)
                res = [spec[c, s, re_rows, :] for s in range(SLOTS)]
                ims = [spec[c, s, im_rows, :] for s in range(SLOTS)]
                z_re = z_im = None
                for s in range(SLOTS):
                    if s < SLOTS - 1:
                        y_re = res[s] + ims[s + 1] if sign > 0 else res[s] - ims[s + 1]
                        y_im = ims[s] - res[s + 1] if sign > 0 else ims[s] + res[s + 1]
                        p_re = res[s] * y_re + ims[s] * y_im
                        p_im = res[s] * y_im - ims[s] * y_re
                        z_im = p_im if z_im is None else z_im + p_im
                    else:
                        p_re = res[s] * res[s] + ims[s] * ims[s]
                    z_re = p_re if z_re is None else z_re + p_re
                if c == 0:
                    zbuf[re_rows, :] = z_re
                    zbuf[im_rows, :] = z_im
                else:
                    zbuf[re_rows, :] = zbuf[re_rows, :] + z_re
                    zbuf[im_rows, :] = zbuf[im_rows, :] + z_im

    def halo(c):
        off = offs[c]

        @pl.when(jnp.logical_not(is_last))
        def _():
            landed(SLOTS, c)
            x = position(SLOTS, c, off)
            if c == 0:
                halo_sq[...] = x * x
            else:
                halo_sq[...] = halo_sq[...] + x * x
            spec[c, 0] = transform(x)
            for sign, base in ((1, 0), (-1, half)):
                @pl.loop(0, half // SUB)
                def _(r):
                    re_rows = pl.ds(pl.multiple_of(base + r * SUB, SUB), SUB)
                    im_rows = pl.ds(pl.multiple_of(bins + base + r * SUB, SUB), SUB)
                    x_re, x_im = spec[c, SLOTS - 1, re_rows, :], spec[c, SLOTS - 1, im_rows, :]
                    y_re, y_im = spec[c, 0, im_rows, :], spec[c, 0, re_rows, :]
                    if sign > 0:
                        zbuf[re_rows, :] = zbuf[re_rows, :] + (x_re * y_re - x_im * y_im)
                        zbuf[im_rows, :] = zbuf[im_rows, :] - (x_re * y_im + x_im * y_re)
                    else:
                        zbuf[re_rows, :] = zbuf[re_rows, :] - (x_re * y_re - x_im * y_im)
                        zbuf[im_rows, :] = zbuf[im_rows, :] + (x_re * y_im + x_im * y_re)

    @pl.when(is_last)
    def _():
        halo_sq[...] = jnp.zeros_like(halo_sq)

    @pl.when(direct)
    def _():
        for c in range(dims):
            take_first(c)

    arrive(0)
    spread(0, rounds)
    arrive(1)
    main(0)
    main(1)
    halo(0)
    arrive(2)
    main(2)
    halo(1)
    halo(2)

    z_hi, z_lo = split(zbuf[...])
    w_hi, w_lo = split(halo_sq[...] - first_sq[...])
    v_hi, v_lo = split(jnp.where(is_last, -last_sq[...], 0.0))
    lag_sum = jnp.dot(inv[...], jnp.concatenate([z_hi, z_lo, z_hi, w_hi, w_lo, v_hi, v_lo], axis=0),
                      preferred_element_type=F32)
    lag_sum = lag_sum + 2.0 * jnp.sum(sum_sq[...], axis=0, keepdims=True)
    by_atom = lag_sum.T
    for g in range(SLOTS):
        for p in range(sub_planes):
            for k in range(2):
                first = p * SLOTS * width + g * width + k * per_owner
                tbuf[2 * (g * sub_planes + p) + k] = by_atom[first:first + per_owner, :]

    @pl.loop(0, quads)
    def _(q):
        @pl.when(q != quad)
        def _():
            pltpu.make_async_remote_copy(
                src_ref=tbuf.at[q], dst_ref=part.at[quad], send_sem=part_send, recv_sem=part_recv,
                device_id=(device(q, chip),), device_id_type=MESH).start()

    part[quad] = tbuf[quad]
    others = pl.ds(0, quads - 1)
    pltpu.make_async_remote_copy(
        src_ref=tbuf.at[others], dst_ref=part.at[others], send_sem=part_send, recv_sem=part_recv,
        device_id=((me + 1) % n,), device_id_type=MESH).wait()
    out[...] = jnp.sum(part[...], axis=0)

    for c in range(dims):
        for o in (3, 1, 2):
            exchange(c, o)[1].wait_send()
        mine, remote, local = exchange(c, 0)

        @pl.when(jnp.logical_not(mine))
        def _():
            remote.wait_send()

        @pl.when(quad > 0)
        def _():
            hand_on(c).wait_send()


def tables(frames):
    f = np.concatenate([np.arange(0, LAGS, 2), np.arange(1, LAGS, 2)]) + 0.5
    t = np.arange(frames)
    angle = 2.0 * np.pi * f[:, None] * t[None, :] / (2 * LAGS)
    fwd = np.concatenate([np.cos(angle), -np.sin(angle)], axis=0).astype(np.float32)
    back = (2.0 * np.pi * f[None, :] * np.arange(LAGS)[:, None]) / (2 * LAGS)
    inv = np.concatenate([np.cos(back), -np.sin(back)], axis=1) * (-2.0 / LAGS)
    inv = inv.astype(np.float32)

    def halves(x):
        hi = x.astype(jnp.bfloat16)
        return hi, (x - hi.astype(np.float32)).astype(jnp.bfloat16)

    k = np.arange(LAGS)[:, None]
    low = (t[None, :] < k).astype(jnp.bfloat16)
    high = (t[None, :] >= frames - k).astype(jnp.bfloat16)
    f_hi, f_lo = halves(fwd)
    i_hi, i_lo = halves(inv)
    return (np.concatenate([f_hi, f_hi, f_lo], axis=1),
            np.concatenate([i_hi, i_hi, i_lo, low, low, high, high], axis=1))


def on_device(n, wrapped, crossings, box_size):
    frames, dims, atoms = wrapped.shape
    per_owner = atoms // n
    quads = n // SLOTS
    assert frames == LAGS and atoms == SLOTS * LANES and n % GROUP == 0 and LANES % (GROUP * per_owner) == 0
    fwd, inv = tables(frames)
    any_spec = pl.BlockSpec(memory_space=pltpu.HBM)
    piece = SUB + dims * frames
    lag_sum = pl.pallas_call(
        functools.partial(kernel, n),
        out_shape=jax.ShapeDtypeStruct((per_owner, LAGS), F32),
        in_specs=[any_spec] * 5,
        out_specs=pl.BlockSpec(memory_space=pltpu.VMEM),
        scratch_shapes=[
            pltpu.VMEM((dims, frames, atoms), F32),
            pltpu.VMEM((dims, frames, atoms), jnp.int32),
            pltpu.VMEM((SLOTS, piece, LANES), F32),
            pltpu.VMEM((SLOTS + 1, piece, LANES), F32),
            pltpu.VMEM(fwd.shape, BF16),
            pltpu.VMEM(inv.shape, BF16),
            pltpu.VMEM((dims, SLOTS, 2 * LAGS, LANES), F32),
            pltpu.VMEM((2 * LAGS, LANES), F32),
            pltpu.VMEM((frames, LANES), F32),
            pltpu.VMEM((frames, LANES), F32),
            pltpu.VMEM((frames, LANES), F32),
            pltpu.VMEM((frames, LANES), F32),
            pltpu.VMEM((quads, per_owner, LAGS), F32),
            pltpu.VMEM((quads, per_owner, LAGS), F32),
            pltpu.SemaphoreType.DMA((dims, 2)),
            pltpu.SemaphoreType.DMA((3,)),
            pltpu.SMEM((dims,), F32),
            pltpu.SemaphoreType.DMA((SLOTS, dims)),
            pltpu.SemaphoreType.DMA((SLOTS + 1, dims)),
            pltpu.SemaphoreType.DMA((dims,)),
            pltpu.SemaphoreType.DMA,
            pltpu.SemaphoreType.DMA,
            pltpu.SemaphoreType.REGULAR,
            pltpu.SemaphoreType.REGULAR,
            pltpu.SemaphoreType.REGULAR,
        ],
        compiler_params=pltpu.CompilerParams(collective_id=0, has_side_effects=True, vmem_limit_bytes=32 * 2**20),
    )(*(pltpu.with_memory_space_constraint(v, pltpu.HBM) for v in (
        jnp.transpose(wrapped, (1, 0, 2)), jnp.transpose(crossings, (1, 0, 2)), box_size,
        jnp.asarray(fwd), jnp.asarray(inv))))
    divisor = (n * frames - jnp.arange(LAGS, dtype=jnp.int32)).astype(F32)
    return lag_sum / divisor[None, :]


def solution(mesh):
    in_specs = (P("tm", None, None), P("tm", None, None), P())
    out_specs = P("tm", None)
    return jax.shard_map(
        functools.partial(on_device, mesh.shape["tm"]), mesh=mesh,
        in_specs=in_specs, out_specs=out_specs, check_vma=False)
```
